512 devices in a mesh: subj: 8 (over z), tr: 64 (over y, x, core).
Axes of the slice: x: 4, y: 8, z: 8, core: 2. Of those that a mesh axis runs over, the one named last changes fastest.
Arguments:
- features: bfloat16 [4096, 2048], P('tr', 'subj'), may hold values from -6 to 6
- block_orders: int32 [4, 64], replicated, may hold values from 0 to 63, each once within a row
- offsets: int32 [4, 4], replicated, may hold values from 0 to 8
- tap_gains: float32 [4, 4], replicated, may hold values from 0.2 to 1
- weights: bfloat16 [8, 2048, 1024], P('subj'), may hold values from -0.125 to 0.125
- signal: bfloat16 [8, 4096, 1024], P('subj', 'tr')
- block_owner: int32 [8, 256, 1], P('subj'), may hold values from 0 to 63; in each aligned block of 256 rows (0 to 255, 256 to 511, ..., all dimensions but the last counted through in order) at most 8 rows name the same one
Outputs:
- energy: float32 [8, 4096, 5], P('subj', 'tr')
- scores: float32 [8, 512, 5], P('subj', 'tr')
The draws below stay inside these ranges and needn't reach their ends.
Inputs may be any that keep to these rules, and one draw needn't show every extreme that they name: `block_orders`: each row names every 4096 block once. `block_owner`: no owner is named by more than 8 voxel blocks of one subject.
All inputs are finite; a program needn't handle non-finite values.
Results may differ from the reference program's by a relative error of at most 0.0003.
Values may be sent and summed in bfloat16 or wider, within the bound.
A program may use at most 64 MiB of HBM per device.

```python
import math
import jax
import jax.numpy as jnp
import numpy as np
from jax import lax

F = 2048
NBAND = 4
NLAG = 4
MAXLAG = 8
NPERM = 4
VB = 4
TRD = 64
NSUBJ = 8
TR = 4096
NB = 256
V = 1024
CAP = 8
SLOTS = 512
KC = 5
N_TR = 64


def draw_offsets(key, part):
    keys = jax.random.split(key, 2)
    taps = jax.random.randint(keys[0], (NBAND * NLAG,), 0, MAXLAG + 1)
    spot = jax.random.randint(keys[1], (), 0, NBAND * NLAG)
    taps = jnp.where(jnp.arange(NBAND * NLAG) == spot, MAXLAG, taps)
    return taps.reshape(NBAND, NLAG).astype(jnp.int32)


def draw_signal(key, part):
    keys = jax.random.split(key, 2)
    times = jnp.arange(TR, dtype=jnp.float32) / (TR - 1)
    base = jax.random.normal(keys[0], (NSUBJ, TR, V), jnp.float32)
    rise = jnp.sqrt(3.0 ** times)
    scale = 0.3 * 10.0 ** jax.random.uniform(keys[1], (NSUBJ, 1, V), jnp.float32)
    return (base * rise[None, :, None] * scale).astype(jnp.bfloat16)


def level_of(own_key, extent, cuts, least, top_value):
    level, own = 1.0, jax.random.fold_in(own_key, 6)
    for position, parts in cuts:
        draws = jnp.exp(jax.random.uniform(jax.random.fold_in(own, position), (parts,), jnp.float32, least / len(cuts), top_value / len(cuts)))
        level = level * jnp.repeat(draws, extent[position] // parts).reshape([-1 if axis == position else 1 for axis in range(len(extent))])
    return level


def routed_block(own_key, own, number, rows, count, top, bound, lean):
    order = jax.random.permutation(own_key, count)
    heavy_load, usual = portions_of(count, rows * top, bound, lean, True), portions_of(count, rows * top, bound, lean, False)
    places = jnp.arange(count)

    def named(sizes, offset_by):
        used = int((sizes > 0).sum())
        fixed = max(1, used // 4)
        passed = fixed + (places - fixed + offset_by * (used - fixed)) % max(1, count - fixed)
        return jnp.zeros((count,), jnp.int32).at[order[jnp.where(places < fixed, places, passed)]].set(jnp.asarray(sizes, jnp.int32))

    sizes = jnp.where(number % 4 == 0, named(heavy_load, number // 4), named(usual, number - number // 4 - 1))
    mixed = jax.random.permutation(jax.random.fold_in(own, 3), count)
    giver, receiver = mixed[0:count // 2 * 2:2], mixed[1:count // 2 * 2:2]
    margin = jnp.minimum(sizes[giver] - 1, bound - sizes[receiver]) // 2
    margin = jnp.where((giver == order[0]) | (receiver == order[0]) | (sizes[receiver] == 0), 0, jnp.maximum(margin, 0))
    passed = jax.random.randint(jax.random.fold_in(own, 4), (count // 2,), 0, 1 << 20) % (margin + 1)
    sizes = sizes.at[giver].add(-passed).at[receiver].add(passed)
    items = jnp.searchsorted(jnp.cumsum(sizes), jnp.arange(rows * top), side="right").astype(jnp.int32)
    table = items.reshape(top, rows).T
    table = table[jax.random.permutation(jax.random.fold_in(own, 1), rows)]
    offset_by = jax.random.randint(jax.random.fold_in(own, 2), (rows, 1), 0, top)
    return jnp.take_along_axis(table, (jnp.arange(top)[None, :] + offset_by) % top, axis=1)


def portions_of(count, total, reach, skew, full):
    weights = [(1 << 20) // math.isqrt(standing ** skew) + 1 for standing in range(1, count + 1)]
    largest = reach if full else min(reach, max(-(-total // count), total * weights[0] // sum(weights)))
    least = 1 if total - largest >= count - 1 else 0
    counts, spare = [largest] + [least] * (count - 1), total - largest - least * (count - 1)
    while spare > 0:
        candidates = [i for i in range(1, count) if counts[i] < largest] or [i for i in range(1, count) if counts[i] < reach]
        whole, budget = sum([weights[i] for i in candidates]), spare
        for i in candidates:
            extra = min(reach - counts[i], max(1, budget * weights[i] // whole), spare)
            counts[i] = counts[i] + extra
            spare = spare - extra
    return np.array(counts)


def gaussian(own_key, shape, spread, most, cuts=(), held_as=jnp.bfloat16):
    array = spread * jax.random.normal(own_key, shape, jnp.float32)
    if cuts:
        array = array * level_of(own_key, shape, cuts, -0.22, 0.18)
    return jnp.clip(array, -most, most).astype(held_as)


def setup_inputs(seed: int = 0) -> dict:
    key_list = jax.random.split(jax.random.key(seed), 8)
    features = gaussian(key_list[0], (TR, F), 1.0, 6.0, ((0, 64), (1, 8)))
    block_orders = jax.vmap(lambda own: jax.random.permutation(own, N_TR))(jax.random.split(key_list[1], NPERM)).reshape((NPERM, N_TR)).astype(jnp.int32)
    offsets = draw_offsets(jax.random.fold_in(key_list[7], 71), 0)
    tap_gains = jnp.clip(jax.random.uniform(key_list[3], (NBAND, NLAG), jnp.float32, 0.2, 1.0), 0.2, 1.0)
    weights = gaussian(key_list[4], (NSUBJ, F, V), F ** -0.5, 0.125, ((0, 8),))
    signal = draw_signal(jax.random.fold_in(key_list[7], 71), 0)
    block_owner_keys = jax.random.split(jax.random.fold_in(key_list[6], 1), NSUBJ * NB // NB)
    block_owner_turns = jax.random.permutation(jax.random.fold_in(key_list[6], 3), NSUBJ * NB // NB)
    block_owner = jax.vmap(lambda own, number: routed_block(jax.random.fold_in(key_list[6], 2), own, number, NB, N_TR, 1, CAP, 2))(block_owner_keys, block_owner_turns).reshape((NSUBJ, NB, 1))
    return {"features": features, "block_orders": block_orders, "offsets": offsets, "tap_gains": tap_gains, "weights": weights, "signal": signal, "block_owner": block_owner}


def filter_series(series, offsets, tap_gains):
    width = F // NBAND
    padded = jnp.concatenate([jnp.zeros((KC, MAXLAG, F), jnp.bfloat16), series], axis=1)
    pieces = []
    for band in range(NBAND):
        part = padded[:, :, band * width:(band + 1) * width]
        total = jnp.zeros((KC, TR, width), jnp.float32)
        for lag in range(NLAG):
            start = (MAXLAG - offsets[band, lag]).astype(jnp.int32)
            total = total + tap_gains[band, lag] * lax.dynamic_slice_in_dim(part, start, TR, 1).astype(jnp.float32)
        pieces.append(total)
    return jnp.concatenate(pieces, axis=2).astype(jnp.bfloat16)


def reference(features, block_orders, offsets, tap_gains, weights, signal, block_owner):
    blocked = features.reshape(N_TR, TRD, F)
    moved = [blocked[block_orders[k]].reshape(TR, F) for k in range(NPERM)]
    series = jnp.stack([features] + moved, axis=0)
    filtered = filter_series(series, offsets, tap_gains).astype(jnp.float32)

    def one_subject(inputs):
        weight, measured, owners = inputs
        predicted = jnp.einsum("ctf,fv->ctv", filtered, weight.astype(jnp.float32))
        values = measured.astype(jnp.float32)
        residual = values[None] - predicted
        squared = residual * residual
        energy = jnp.mean(squared, axis=2).T
        rss = jnp.sum(squared, axis=1)
        tss = jnp.sum(values * values, axis=0)
        fit = jnp.log((rss + 1e-6) / (tss + 1e-6)[None, :])
        block_fit = jnp.mean(fit.reshape(KC, NB, VB), axis=2).T
        owner_list = owners[:, 0].astype(jnp.int32)
        order = jnp.arange(NB, dtype=jnp.int32)
        rank = jnp.sum(((owner_list[:, None] == owner_list[None, :]) & (order[:, None] > order[None, :])).astype(jnp.int32), axis=1)
        slot = (owner_list * CAP + rank).astype(jnp.int32)
        scores = jnp.zeros((SLOTS, KC), jnp.float32).at[slot].set(block_fit)
        return energy, scores

    return lax.map(one_subject, (weights, signal, block_owner))
```

```python
import jax
import jax.numpy as jnp
from jax import lax
from jax.experimental import pallas as pl
from jax.experimental.pallas import tpu as pltpu
from jax.sharding import PartitionSpec as P

MAXLAG = 8
NLAG = 4
VB = 4
CAP = 8
NT = 64
NZ = 8
NY = 8
NX = 8
KC = 5
ROWS = 64
FZ = 256
F = 2048
V = 1024
BAND_DEVICES = 2
LANES = 128
VT = V // LANES
EPS = 1e-06

MESH = pl.DeviceIdType.MESH
F32 = jnp.float32
BF16 = jnp.bfloat16


def dot(a, b):
    return jnp.dot(a, b, preferred_element_type=F32)


def iota(shape, axis):
    return lax.broadcasted_iota(jnp.int32, shape, axis)


def wait_for(ref, sem):
    pltpu.make_async_copy(ref, ref, sem).wait()


def kernel(
    feat_hbm, orders, offs, gains, w_hbm, sig_hbm, owner,
    energy, scores,
    feat, sig, w, pad, send_f, recv_f, zbuf, rim, wide, send_s, recv_s, sall, pred,
    send_r, recv_r, c1_send, c1_recv, c2, c3, sel,
    local_sem, rim_ss, rim_rs, f_ss, f_rs, s_ss, s_rs, z_ss, z_rs, r_ss, r_rs,
    c1_ss, c1_rs, c2_ss, c2_rs, c3_ss, c3_rs,
):
    z = lax.axis_index("subj")
    me = lax.axis_index("tr")
    y = me // NX
    xc = me % NX

    def send(src, dst, ss, rs, **where):
        pltpu.make_async_remote_copy(
            src_ref=src, dst_ref=dst, send_sem=ss, recv_sem=rs,
            device_id=where, device_id_type=MESH,
        ).start()

    feat_copy = pltpu.make_async_copy(feat_hbm, feat, local_sem.at[0])
    sig_copy = pltpu.make_async_copy(sig_hbm.at[0], sig, local_sem.at[1])
    w_copy = pltpu.make_async_copy(w_hbm.at[0], w, local_sem.at[2])
    feat_copy.start()
    sig_copy.start()
    w_copy.start()

    barrier = pltpu.get_barrier_semaphore()

    def greet_tr(i, carry):
        pl.semaphore_signal(barrier, inc=1, device_id={"tr": (me + i) % NT}, device_id_type=MESH)
        return carry

    def greet_subj(i, carry):
        pl.semaphore_signal(barrier, inc=1, device_id={"subj": (z + i) % NZ}, device_id_type=MESH)
        return carry

    lax.fori_loop(1, NZ, greet_subj, 0)
    lax.fori_loop(1, NT, greet_tr, 0)

    feat_copy.wait()
    pad[0:MAXLAG] = jnp.zeros((MAXLAG, FZ), F32)
    pad[MAXLAG + ROWS:] = jnp.zeros((MAXLAG, FZ), F32)
    pad[MAXLAG:MAXLAG + ROWS] = feat[...].astype(F32)
    band = z // BAND_DEVICES
    total = jnp.zeros((ROWS + MAXLAG, FZ), F32)
    for lag in range(MAXLAG + 1):
        gain = jnp.float32(0.0)
        for tap in range(NLAG):
            gain = gain + jnp.where(offs[band, tap] == lag, gains[band, tap], jnp.float32(0.0))
        total = total + gain * pad[MAXLAG - lag:MAXLAG - lag + ROWS + MAXLAG]
    for j in range(FZ // LANES):
        send_f[:, j, :] = total[:ROWS, j * LANES:(j + 1) * LANES]
    rim[z] = total[ROWS:].astype(BF16)

    pl.semaphore_wait(barrier, NT - 1 + NZ - 1)

    def send_rim(i, carry):
        send(rim.at[z], rim.at[z], rim_ss, rim_rs, subj=(z + i) % NZ)
        return carry

    def send_feature(i, carry):
        to = (me + i) % NT
        send(send_f.at[to], recv_f.at[me], f_ss, f_rs, tr=to)
        return carry

    lax.fori_loop(1, NT, send_feature, 0)
    lax.fori_loop(1, NZ, send_rim, 0)
    recv_f[me] = send_f[me]

    sig_copy.wait()
    for j in range(VT):
        wide[:, j, :] = sig[:, j * LANES:(j + 1) * LANES].astype(F32)
    send_s[...] = wide[...].astype(BF16)

    def send_signal(i, carry):
        to = (me + i) % NT
        send(send_s.at[to], recv_s.at[me], s_ss, s_rs, tr=to)
        return carry

    lax.fori_loop(1, NT, send_signal, 0)
    recv_s[me] = send_s[me]

    wait_for(recv_f.at[pl.ds(0, NT - 1)], f_rs)
    for j in range(FZ // LANES):
        zbuf[z, :, j * LANES:(j + 1) * LANES] = recv_f[:, j, :].astype(BF16)

    def send_columns(i, carry):
        to = (z + i) % NZ
        send(zbuf.at[z], zbuf.at[z], z_ss, z_rs.at[z], subj=to)
        return carry

    lax.fori_loop(1, NZ, send_columns, 0)

    wait_for(rim.at[pl.ds(0, NZ - 1)], rim_rs)
    w_copy.wait()
    part = dot(rim[0], w[0:FZ])
    for k in range(1, NZ):
        part = part + dot(rim[k], w[k * FZ:(k + 1) * FZ])
    for j in range(VT):
        send_r[:, j, :] = part[:, j * LANES:(j + 1) * LANES]

    def send_part(i, carry):
        @pl.when(i != me)
        def _():
            send(send_r.at[i], recv_r.at[me], r_ss, r_rs, tr=i)
        return carry

    lax.fori_loop(0, MAXLAG, send_part, 0)

    @pl.when(me < MAXLAG)
    def _():
        recv_r[me] = send_r[me]

    blocks = owner.shape[1]
    owned = jnp.broadcast_to(owner[...] == me, (CAP, blocks))
    before = (iota((blocks, blocks), 0) < iota((blocks, blocks), 1)).astype(F32).astype(BF16)
    rank = dot(owned.astype(F32).astype(BF16), before)
    chosen = jnp.where(owned & (rank == iota((CAP, blocks), 0).astype(F32)), 1.0, 0.0).astype(BF16)
    spread = (iota((blocks, V), 1) // VB == iota((blocks, V), 0)).astype(F32).astype(BF16)
    sel[...] = dot(chosen, spread)

    def place(c):
        if c == 0:
            return iota((NT, NT), 0) == iota((NT, NT), 1)
        return jnp.broadcast_to(orders[c - 1:c, :], (NT, NT)) == iota((NT, NT), 0)

    wait_for(recv_s.at[pl.ds(0, NT - 1)], s_rs)
    wide[...] = recv_s[...].astype(F32)
    tss = []
    for j in range(VT):
        column = wide[:, j, :]
        sall[0, :, j * LANES:(j + 1) * LANES] = column
        tss.append(jnp.sum(column * column, axis=0, keepdims=True))
    rows = sall[0].astype(BF16)
    for c in range(1, KC):
        sall[c] = dot(place(c).astype(F32).astype(BF16), rows)

    @pl.when(me < MAXLAG)
    def _():
        wait_for(recv_r.at[pl.ds(0, NT - 1)], r_rs)
        after = (iota((NT, NT), 0) == iota((NT, NT), 1) + 1).astype(F32).astype(BF16)
        for j in range(VT):
            pred[:, j * LANES:(j + 1) * LANES] = recv_r[:, j, :]
        high = pred[...].astype(BF16)
        low = (pred[...] - high.astype(F32)).astype(BF16)
        for c in range(KC):
            placed = place(c).astype(F32).astype(BF16)
            shifted = dot(placed, after).astype(BF16)
            behind = lax.dot_general(
                shifted, placed, (((1,), (1,)), ((), ())), preferred_element_type=F32
            ).astype(BF16)
            sall[c] = sall[c] - (dot(behind, high) + dot(behind, low))

    def weight(k):
        return w[pl.ds(pl.multiple_of(k * FZ, FZ), FZ), :]

    pred[...] = dot(zbuf[z], weight(z))
    for i in (1, 7, 2, 6, 3, 5, 4):
        k = (z + i) % NZ
        wait_for(zbuf.at[k], z_rs.at[k])
        pred[...] += dot(zbuf[k], weight(k))

    over = [jnp.zeros((NT, LANES), F32) for _ in range(KC)]
    for j in range(VT):
        value = pred[:, j * LANES:(j + 1) * LANES]
        stats = []
        for c in range(KC):
            residual = sall[c, :, j * LANES:(j + 1) * LANES] - value
            squared = residual * residual
            over[c] = over[c] + squared
            stats.append(jnp.sum(squared, axis=0, keepdims=True))
        stats = stats + [tss[j], jnp.zeros((2, LANES), F32)]
        c1_send[j, 0:8, :] = jnp.concatenate(stats, axis=0)
    placed_energy = []
    for c in range(KC):
        column = jnp.sum(over[c], axis=1, keepdims=True)
        placed_energy.append(
            jnp.sum(jnp.where(place(c), jnp.broadcast_to(column, (NT, NT)), 0.0), axis=0, keepdims=True)
        )
    placed_energy = jnp.concatenate(placed_energy + [jnp.zeros((3, NT), F32)], axis=0)
    placed_energy = jnp.concatenate([placed_energy, jnp.zeros((8, LANES - NT), F32)], axis=1)
    for j in range(NY):
        c1_send[j, 8:16, :] = placed_energy

    def send_c1(i, carry):
        to = (y + i) % NY
        send(c1_send.at[to], c1_recv.at[y], c1_ss, c1_rs, tr=to * NX + xc)
        return carry

    lax.fori_loop(1, NY, send_c1, 0)
    c1_recv[y] = c1_send[y]
    wait_for(c1_recv.at[pl.ds(0, NY - 1)], c1_rs)
    lane = iota((8, LANES), 1)
    tile = c1_recv[0, 0:8, :]
    for k in range(1, NY):
        tile = tile + c1_recv[k, 0:8, :]
    packed = jnp.zeros((8, LANES), F32)
    for k in range(NY):
        moved = pltpu.roll(c1_recv[k, 8:16, :], ((k - y) * NX + LANES) % LANES, 1)
        packed = jnp.where(lane // NX == k, moved, packed)
    c2[xc, 0:8, :] = tile
    c2[xc, 8:16, :] = packed

    def send_c2(i, carry):
        send(c2.at[xc], c2.at[xc], c2_ss, c2_rs, tr=y * NX + (xc + i) % NX)
        return carry

    lax.fori_loop(1, NX, send_c2, 0)
    wait_for(c2.at[pl.ds(0, NX - 1)], c2_rs)
    tile = c2[0, 0:8, :]
    for k in range(1, NX):
        tile = tile + c2[k, 0:8, :]
    fit = jnp.log((tile + EPS) / (tile[KC:KC + 1] + EPS))
    c3[y] = fit

    def send_c3(i, carry):
        send(c3.at[y], c3.at[y], c3_ss, c3_rs, tr=((y + i) % NY) * NX + xc)
        return carry

    lax.fori_loop(1, NY, send_c3, 0)

    mean = jnp.zeros((8, LANES), F32)
    for k in range(NX):
        moved = pltpu.roll(c2[k, 8:16, :], (k - xc + LANES) % LANES, 1)
        mean = jnp.where(lane % NX == k, moved, mean)
    mean = mean * (1.0 / V)
    for c in range(KC):
        energy[c, :, :] = mean[c:c + 1, :NT]

    wait_for(c3.at[pl.ds(0, NY - 1)], c3_rs)
    result = jnp.zeros((8, LANES), F32)
    for k in range(CAP):
        picked = jnp.zeros((8, LANES), F32)
        for j in range(NY):
            picked = picked + c3[j] * sel[k:k + 1, j * LANES:(j + 1) * LANES]
        column = jnp.sum(picked, axis=1, keepdims=True)
        result = jnp.where(lane == k, jnp.broadcast_to(column, (8, LANES)), result)
    result = result * (1.0 / VB)
    for c in range(KC):
        scores[c, :, :] = result[c:c + 1, :CAP]

    wait_for(rim.at[pl.ds(0, NZ - 1)], rim_ss)
    wait_for(send_f.at[pl.ds(0, NT - 1)], f_ss)
    wait_for(send_s.at[pl.ds(0, NT - 1)], s_ss)
    wait_for(zbuf.at[pl.ds(0, NZ - 1)], z_ss)
    wait_for(c1_send.at[pl.ds(0, NY - 1)], c1_ss)
    wait_for(c2.at[pl.ds(0, NX - 1)], c2_ss)
    wait_for(c3.at[pl.ds(0, NY - 1)], c3_ss)

    @pl.when(me < MAXLAG)
    def _():
        wait_for(send_r.at[pl.ds(0, MAXLAG - 1)], r_ss)

    @pl.when(me >= MAXLAG)
    def _():
        wait_for(send_r, r_ss)


def on_device(features, block_orders, offsets, tap_gains, weights, signal, block_owner):
    anywhere = pl.BlockSpec(memory_space=pl.ANY)
    vmem = pl.BlockSpec(memory_space=pltpu.VMEM)
    smem = pl.BlockSpec(memory_space=pltpu.SMEM)
    sem = pltpu.SemaphoreType.DMA
    owner = block_owner.reshape(1, block_owner.shape[1])
    energy, scores = pl.pallas_call(
        kernel,
        out_shape=(
            jax.ShapeDtypeStruct((KC, 1, NT), F32),
            jax.ShapeDtypeStruct((KC, 1, CAP), F32),
        ),
        in_specs=[anywhere, vmem, smem, smem, anywhere, anywhere, vmem],
        out_specs=(vmem, vmem),
        scratch_shapes=[
            pltpu.VMEM((ROWS, FZ), BF16),
            pltpu.VMEM((ROWS, V), BF16),
            pltpu.VMEM((F, V), BF16),
            pltpu.VMEM((ROWS + 2 * MAXLAG, FZ), F32),
            pltpu.VMEM((NT, FZ // LANES, LANES), F32),
            pltpu.VMEM((NT, FZ // LANES, LANES), F32),
            pltpu.VMEM((NZ, NT, FZ), BF16),
            pltpu.VMEM((NZ, MAXLAG, FZ), BF16),
            pltpu.VMEM((NT, VT, LANES), F32),
            pltpu.VMEM((NT, VT, LANES), BF16),
            pltpu.VMEM((NT, VT, LANES), BF16),
            pltpu.VMEM((KC, NT, V), F32),
            pltpu.VMEM((NT, V), F32),
            pltpu.VMEM((MAXLAG, VT, LANES), F32),
            pltpu.VMEM((NT, VT, LANES), F32),
            pltpu.VMEM((NY, 16, LANES), F32),
            pltpu.VMEM((NY, 16, LANES), F32),
            pltpu.VMEM((NX, 16, LANES), F32),
            pltpu.VMEM((NY, 8, LANES), F32),
            pltpu.VMEM((CAP, V), F32),
            sem((3,)),
            sem, sem, sem, sem, sem, sem, sem, sem((NZ,)), sem, sem,
            sem, sem, sem, sem, sem, sem,
        ],
        compiler_params=pltpu.CompilerParams(
            collective_id=0, has_side_effects=True, vmem_limit_bytes=40 * 1024 * 1024
        ),
    )(features, block_orders, offsets, tap_gains, weights, signal, owner)
    return jnp.transpose(energy, (1, 2, 0)), jnp.transpose(scores, (1, 2, 0))


def solution(mesh):
    placed = (
        P("tr", "subj"),
        P(),
        P(),
        P(),
        P("subj", None, None),
        P("subj", "tr", None),
        P("subj", None, None),
    )
    return jax.shard_map(
        on_device,
        mesh=mesh,
        in_specs=placed,
        out_specs=(P("subj", "tr", None), P("subj", "tr", None)),
        check_vma=False,
    )
```

```python
import jax
import jax.numpy as jnp
from jax import lax
from jax.experimental import pallas as pl
from jax.experimental.pallas import tpu as pltpu
from jax.sharding import PartitionSpec as P

MAXLAG = 8
NLAG = 4
VB = 4
CAP = 8
NT = 64
NZ = 8
NY = 8
NX = 8
KC = 5
ROWS = 64
FZ = 256
F = 2048
V = 1024
BAND_DEVICES = 2
LANES = 128
VT = V // LANES
EPS = 1e-06

MESH = pl.DeviceIdType.MESH
F32 = jnp.float32
BF16 = jnp.bfloat16


def dot(a, b):
    return jnp.dot(a, b, preferred_element_type=F32)


def iota(shape, axis):
    return lax.broadcasted_iota(jnp.int32, shape, axis)


def wait_for(ref, sem):
    pltpu.make_async_copy(ref, ref, sem).wait()


def kernel(
    feat_hbm, orders_hbm, offs_hbm, gains_hbm, w_hbm, sig_hbm, owner_hbm,
    energy, scores,
    orders, offs, gains, owner, feat, sig, w, pad, send_f, recv_f, zbuf, rim, wide, send_s, recv_s, sall, pred,
    send_r, recv_r, by_owner, kept, lhs, send_m, recv_m,
    local_sem, rim_ss, rim_rs, f_ss, f_rs, s_ss, s_rs, z_ss, z_rs, r_ss, r_rs,
    m_ss, m_rs,
):
    z = lax.axis_index("subj")
    me = lax.axis_index("tr")
    y = me // NX
    xc = me % NX

    def send(src, dst, ss, rs, **where):
        pltpu.make_async_remote_copy(
            src_ref=src, dst_ref=dst, send_sem=ss, recv_sem=rs,
            device_id=where, device_id_type=MESH,
        ).start()

    leaving = []

    feat_copy = pltpu.make_async_copy(feat_hbm, feat, local_sem.at[0])
    offs_copy = pltpu.make_async_copy(offs_hbm, offs, local_sem.at[3])
    gains_copy = pltpu.make_async_copy(gains_hbm, gains, local_sem.at[4])
    sig_copy = pltpu.make_async_copy(sig_hbm.at[0], sig, local_sem.at[1])
    orders_copy = pltpu.make_async_copy(orders_hbm, orders, local_sem.at[5])
    owner_copy = pltpu.make_async_copy(owner_hbm, owner, local_sem.at[6])
    w_copy = pltpu.make_async_copy(w_hbm.at[0], w, local_sem.at[2])
    for copy in (feat_copy, offs_copy, gains_copy, sig_copy, orders_copy, owner_copy, w_copy):
        copy.start()

    barrier = pltpu.get_barrier_semaphore()

    def greet_tr(i, carry):
        pl.semaphore_signal(barrier, inc=1, device_id={"tr": (me + i) % NT}, device_id_type=MESH)
        return carry

    def greet_subj(i, carry):
        pl.semaphore_signal(barrier, inc=1, device_id={"subj": (z + i) % NZ}, device_id_type=MESH)
        return carry

    lax.fori_loop(1, NZ, greet_subj, 0)
    lax.fori_loop(1, NT, greet_tr, 0)

    feat_copy.wait()
    offs_copy.wait()
    gains_copy.wait()
    pad[0:MAXLAG] = jnp.zeros((MAXLAG, FZ), F32)
    pad[MAXLAG + ROWS:] = jnp.zeros((MAXLAG, FZ), F32)
    pad[MAXLAG:MAXLAG + ROWS] = feat[...].astype(F32)
    band = z // BAND_DEVICES
    total = jnp.zeros((ROWS + MAXLAG, FZ), F32)
    for lag in range(MAXLAG + 1):
        gain = jnp.float32(0.0)
        for tap in range(NLAG):
            gain = gain + jnp.where(offs[band, tap] == lag, gains[band, tap], jnp.float32(0.0))
        total = total + gain * pad[MAXLAG - lag:MAXLAG - lag + ROWS + MAXLAG]
    for j in range(FZ // LANES):
        send_f[:, j, :] = total[:ROWS, j * LANES:(j + 1) * LANES]
    rim[z] = total[ROWS:].astype(BF16)

    pl.semaphore_wait(barrier, NT - 1 + NZ - 1)

    def send_rim(i, carry):
        send(rim.at[z], rim.at[z], rim_ss, rim_rs, subj=(z + i) % NZ)
        return carry

    def send_feature(i, carry):
        to = (me + i) % NT
        send(send_f.at[to], recv_f.at[me], f_ss, f_rs, tr=to)
        return carry

    lax.fori_loop(1, NT, send_feature, 0)
    leaving.append((send_f.at[pl.ds(0, NT - 1)], f_ss))
    lax.fori_loop(1, NZ, send_rim, 0)
    leaving.append((rim.at[pl.ds(0, NZ - 1)], rim_ss))
    recv_f[me] = send_f[me]

    sig_copy.wait()
    for j in range(VT):
        wide[:, j, :] = sig[:, j * LANES:(j + 1) * LANES].astype(F32)
    send_s[...] = wide[...].astype(BF16)

    def send_signal(i, carry):
        to = (me + i) % NT
        send(send_s.at[to], recv_s.at[me], s_ss, s_rs, tr=to)
        return carry

    lax.fori_loop(1, NT, send_signal, 0)
    leaving.append((send_s.at[pl.ds(0, NT - 1)], s_ss))
    recv_s[me] = send_s[me]

    orders_copy.wait()
    owner_copy.wait()
    blocks = owner.shape[1]
    wide_lanes = 2 * LANES
    named = (jnp.broadcast_to(owner[...], (NT, blocks)) == iota((NT, blocks), 0)).astype(F32).astype(BF16)
    spread = ((iota((blocks, V), 1) >> 2) == iota((blocks, V), 0)).astype(F32).astype(BF16)
    by_owner[...] = dot(named, spread).astype(BF16)
    same = lax.dot_general(named, named, (((0,), (0,)), ((), ())), preferred_element_type=F32)
    rank = jnp.sum(
        jnp.where(iota((blocks, blocks), 1) < iota((blocks, blocks), 0), same, 0.0), axis=1, keepdims=True
    )
    slot = ((iota((blocks, wide_lanes), 1) & 31) >> 2).astype(F32)
    ranked = (jnp.broadcast_to(rank, (blocks, wide_lanes)) == slot).astype(F32).astype(BF16)
    gathered = ((iota((V, blocks), 0) >> 2) == iota((V, blocks), 1)).astype(F32).astype(BF16)
    places = dot(gathered, ranked)
    lane = iota((V, wide_lanes), 1)
    places = jnp.where((iota((V, wide_lanes), 0) & 3) == (lane & 3), places, 0.0)
    for c in range(KC + 1):
        kept[c * V:(c + 1) * V] = jnp.where((lane >> 5) == c, places, 0.0).astype(BF16)
    mine = jnp.sum(jnp.where(owner[...] == me, 1.0, 0.0), axis=1, keepdims=True)

    wait_for(recv_f.at[pl.ds(0, NT - 1)], f_rs)
    for j in range(FZ // LANES):
        zbuf[z, :, j * LANES:(j + 1) * LANES] = recv_f[:, j, :].astype(BF16)

    def send_columns(i, carry):
        to = (z + i) % NZ
        send(zbuf.at[z], zbuf.at[z], z_ss, z_rs.at[z], subj=to)
        return carry

    lax.fori_loop(1, NZ, send_columns, 0)
    leaving.append((zbuf.at[pl.ds(0, NZ - 1)], z_ss))

    wait_for(rim.at[pl.ds(0, NZ - 1)], rim_rs)
    w_copy.wait()
    part = dot(rim[0], w[0:FZ])
    for k in range(1, NZ):
        part = part + dot(rim[k], w[k * FZ:(k + 1) * FZ])
    for j in range(VT):
        send_r[:, j, :] = part[:, j * LANES:(j + 1) * LANES]

    def send_part(i, carry):
        @pl.when(i != me)
        def _():
            send(send_r.at[i], recv_r.at[me], r_ss, r_rs, tr=i)
        return carry

    lax.fori_loop(0, MAXLAG, send_part, 0)

    @pl.when(me < MAXLAG)
    def _():
        recv_r[me] = send_r[me]

    def place(c):
        if c == 0:
            return iota((NT, NT), 0) == iota((NT, NT), 1)
        return jnp.broadcast_to(orders[c - 1:c, :], (NT, NT)) == iota((NT, NT), 0)

    def keep(c, j, value):
        columns = pl.ds(c * V + j * LANES, LANES)
        holds = by_owner[:, j * LANES:(j + 1) * LANES].astype(F32)
        for part in range(3):
            high = value.astype(BF16).astype(F32)
            lhs[part * NT:(part + 1) * NT, columns] = (holds * high).astype(BF16)
            value = value - high

    wait_for(recv_s.at[pl.ds(0, NT - 1)], s_rs)
    wide[...] = recv_s[...].astype(F32)
    for j in range(VT):
        column = wide[:, j, :]
        sall[0, :, j * LANES:(j + 1) * LANES] = column
        keep(KC, j, jnp.sum(column * column, axis=0, keepdims=True))
    rows = sall[0].astype(BF16)
    for c in range(1, KC):
        sall[c] = dot(place(c).astype(F32).astype(BF16), rows)

    @pl.when(me < MAXLAG)
    def _():
        wait_for(recv_r.at[pl.ds(0, NT - 1)], r_rs)
        after = (iota((NT, NT), 0) == iota((NT, NT), 1) + 1).astype(F32).astype(BF16)
        for j in range(VT):
            pred[:, j * LANES:(j + 1) * LANES] = recv_r[:, j, :]
        high = pred[...].astype(BF16)
        low = (pred[...] - high.astype(F32)).astype(BF16)
        for c in range(KC):
            placed = place(c).astype(F32).astype(BF16)
            shifted = dot(placed, after).astype(BF16)
            behind = lax.dot_general(
                shifted, placed, (((1,), (1,)), ((), ())), preferred_element_type=F32
            ).astype(BF16)
            sall[c] = sall[c] - (dot(behind, high) + dot(behind, low))

    def weight(k):
        return w[pl.ds(pl.multiple_of(k * FZ, FZ), FZ), :]

    pred[...] = dot(zbuf[z], weight(z))
    for i in (1, 7, 2, 6, 3, 5, 4):
        k = (z + i) % NZ
        wait_for(zbuf.at[k], z_rs.at[k])
        pred[...] += dot(zbuf[k], weight(k))

    over = [jnp.zeros((NT, LANES), F32) for _ in range(KC)]
    for j in range(VT):
        value = pred[:, j * LANES:(j + 1) * LANES]
        for c in range(KC):
            residual = sall[c, :, j * LANES:(j + 1) * LANES] - value
            squared = residual * residual
            over[c] = over[c] + squared
            keep(c, j, jnp.sum(squared, axis=0, keepdims=True))
    parts = dot(lhs[...], kept[...])
    message = parts[:NT] + parts[NT:2 * NT] + parts[2 * NT:]
    low, high = message[:, :LANES], message[:, LANES:]
    diagonal = iota((NT, NT), 0) == iota((NT, NT), 1)
    for c in range(KC):
        column = jnp.broadcast_to(jnp.sum(over[c], axis=1, keepdims=True), (NT, NT))
        row = jnp.sum(jnp.where(place(c), column, 0.0), axis=0, keepdims=True)
        column = jnp.sum(jnp.where(diagonal, jnp.broadcast_to(row, (NT, NT)), 0.0), axis=1, keepdims=True)
        high = jnp.where(iota((NT, LANES), 1) == 64 + c, jnp.broadcast_to(column, (NT, LANES)), high)
    send_m[:, 0, :] = low
    send_m[:, 1, :] = high

    def send_message(i, carry):
        to = (me + i) % NT
        send(send_m.at[to], recv_m.at[me], m_ss, m_rs, tr=to)
        return carry

    lax.fori_loop(1, NT, send_message, 0)
    leaving.append((send_m.at[pl.ds(0, NT - 1)], m_ss))
    recv_m[me] = send_m[me]
    wait_for(recv_m.at[pl.ds(0, NT - 1)], m_rs)

    high = recv_m[:, 1, :]
    turned = jnp.transpose(high) * (1.0 / V)
    for c in range(KC):
        energy[c, :, :] = turned[64 + c:65 + c, :]
    sums = [jnp.sum(recv_m[:, 0, :], axis=0, keepdims=True), jnp.sum(high, axis=0, keepdims=True)]
    sums = [sums[c // 4][:, (c % 4) * 32:(c % 4) * 32 + 32] for c in range(KC + 1)]
    fit = jnp.log((jnp.concatenate(sums[:KC], axis=0) + EPS) / (sums[KC] + EPS))
    small = iota((KC, 32), 1)
    result = jnp.zeros((KC, 32), F32)
    for k in range(CAP):
        column = jnp.sum(jnp.where((small >> 2) == k, fit, 0.0), axis=1, keepdims=True)
        result = jnp.where(small == k, jnp.broadcast_to(column, (KC, 32)), result)
    result = jnp.where(small.astype(F32) < jnp.broadcast_to(mine, (KC, 32)), result * (1.0 / VB), 0.0)
    for c in range(KC):
        scores[c, :, :] = result[c:c + 1, :CAP]

    for ref, sem in leaving:
        wait_for(ref, sem)

    @pl.when(me < MAXLAG)
    def _():
        wait_for(send_r.at[pl.ds(0, MAXLAG - 1)], r_ss)

    @pl.when(me >= MAXLAG)
    def _():
        wait_for(send_r, r_ss)


def on_device(features, block_orders, offsets, tap_gains, weights, signal, block_owner):
    hbm = pl.BlockSpec(memory_space=pltpu.HBM)
    vmem = pl.BlockSpec(memory_space=pltpu.VMEM)
    sem = pltpu.SemaphoreType.DMA
    owner = block_owner.reshape(1, block_owner.shape[1])
    energy, scores = pl.pallas_call(
        kernel,
        out_shape=(
            jax.ShapeDtypeStruct((KC, 1, NT), F32),
            jax.ShapeDtypeStruct((KC, 1, CAP), F32),
        ),
        in_specs=[hbm] * 7,
        out_specs=(vmem, vmem),
        scratch_shapes=[
            pltpu.VMEM((KC - 1, NT), jnp.int32),
            pltpu.SMEM(offsets.shape, jnp.int32),
            pltpu.SMEM(tap_gains.shape, F32),
            pltpu.VMEM(owner.shape, jnp.int32),
            pltpu.VMEM((ROWS, FZ), BF16),
            pltpu.VMEM((ROWS, V), BF16),
            pltpu.VMEM((F, V), BF16),
            pltpu.VMEM((ROWS + 2 * MAXLAG, FZ), F32),
            pltpu.VMEM((NT, FZ // LANES, LANES), F32),
            pltpu.VMEM((NT, FZ // LANES, LANES), F32),
            pltpu.VMEM((NZ, NT, FZ), BF16),
            pltpu.VMEM((NZ, MAXLAG, FZ), BF16),
            pltpu.VMEM((NT, VT, LANES), F32),
            pltpu.VMEM((NT, VT, LANES), BF16),
            pltpu.VMEM((NT, VT, LANES), BF16),
            pltpu.VMEM((KC, NT, V), F32),
            pltpu.VMEM((NT, V), F32),
            pltpu.VMEM((MAXLAG, VT, LANES), F32),
            pltpu.VMEM((NT, VT, LANES), F32),
            pltpu.VMEM((NT, V), BF16),
            pltpu.VMEM(((KC + 1) * V, 2 * LANES), BF16),
            pltpu.VMEM((3 * NT, (KC + 1) * V), BF16),
            pltpu.VMEM((NT, 2, LANES), F32),
            pltpu.VMEM((NT, 2, LANES), F32),
            sem((7,)),
            sem, sem, sem, sem, sem, sem, sem, sem((NZ,)), sem, sem,
            sem, sem,
        ],
        compiler_params=pltpu.CompilerParams(
            collective_id=0, has_side_effects=True, vmem_limit_bytes=58 * 1024 * 1024
        ),
    )(features, block_orders, offsets, tap_gains, weights, signal, owner)
    return jnp.transpose(energy, (1, 2, 0)), jnp.transpose(scores, (1, 2, 0))


def solution(mesh):
    placed = (
        P("tr", "subj"),
        P(),
        P(),
        P(),
        P("subj", None, None),
        P("subj", "tr", None),
        P("subj", None, None),
    )
    return jax.shard_map(
        on_device,
        mesh=mesh,
        in_specs=placed,
        out_specs=(P("subj", "tr", None), P("subj", "tr", None)),
        check_vma=False,
    )
```
